32 devices in a mesh: dp: 8 (over z, y), mp: 4 (over x, core).
Axes of the slice: x: 2, y: 2, z: 4, core: 2. Of those that a mesh axis runs over, the one named last changes fastest.
Arguments:
- output_gradient: bfloat16 [1536, 3584], P('dp', 'mp'), may hold values from -6 to 6
- gate_preactivation: bfloat16 [1536, 9984], P('dp', 'mp'), may hold values from -8 to 8
- up_preactivation: bfloat16 [1536, 9984], P('dp', 'mp'), may hold values from -6 to 6
- down_weight: bfloat16 [9984, 3584], P('mp'), may hold values from -0.0625 to 0.0625
- adapter_first: bfloat16 [9984, 96], P('mp'), may hold values from -0.0625 to 0.0625
- adapter_second: bfloat16 [96, 3584], replicated, may hold values from -0.09375 to 0.09375
- plan: int32 [192], P('dp'), may hold values from 0 to 7, as said below
Outputs:
- grad_gate: bfloat16 [1536, 9984], P('dp', 'mp')
- grad_up: bfloat16 [1536, 9984], P('dp', 'mp')
- grad_a: float32 [4, 2496, 96], P('mp', 'dp')
- grad_b: float32 [96, 3584], P('dp')
The draws below stay inside these ranges and needn't reach their ends.
Inputs may be any that keep to these rules, and one draw needn't show every extreme that they name: Every owner 0 to 7 is named by exactly 24 blocks; of the 24 blocks of one device (plan rows of one index of dp) at most 3 name the same owner, and in every draw some device's blocks name one owner exactly 3 times.
All inputs are finite; a program needn't handle non-finite values.
Results may differ from the reference program's by a relative error of at most 0.005.
Values may be sent and summed in bfloat16 or wider, within the bound.
No kernel may reach another device: no remote copies, remote signals or barrier semaphores. Data moves between devices by JAX's collectives and lax.ppermute only.
A program may use at most 64 MiB of HBM per device.

```python
import jax
import jax.numpy as jnp
from jax import lax

MODEL_WIDTH = 3584
HIDDEN_SHARE = 9984
ADAPTER_RANK = 96
OWN = 24
CAP = 3
TOKENS = 1536
N_DP = 8
N_MP = 4


def draw_plan(key, part):
    key_shift = jax.random.fold_in(key, 11)
    key_slots = jax.random.fold_in(key, 23)
    key_label = jax.random.fold_in(key, 37)
    shift_order = jax.random.permutation(key_shift, N_DP)
    shifts = shift_order[jnp.arange(OWN) // CAP]
    slot_keys = jax.random.split(key_slots, N_DP)
    slot_perm = jax.vmap(lambda single: jax.random.permutation(single, OWN))(slot_keys)
    relabel = jax.random.permutation(key_label, N_DP)
    sources = jnp.arange(N_DP)[:, None]
    virtual = (sources + shifts[slot_perm]) % N_DP
    owners = relabel[virtual]
    return owners.reshape(-1).astype(jnp.int32)


def steps_of(own_key, extent, shards, smallest, largest):
    def one(axis_at, blocks):
        steps = jax.random.uniform(jax.random.fold_in(jax.random.fold_in(own_key, 6), axis_at), (blocks,), jnp.float32, smallest / len(shards), largest / len(shards))
        return jnp.repeat(jnp.exp(steps), extent[axis_at] // blocks).reshape((-1,) + (1,) * (len(extent) - axis_at - 1))

    loudness = one(*shards[0])
    for cut in shards[1:]:
        loudness = loudness * one(*cut)
    return loudness


def centred(stream_key, dims, spread, most, cuts=(), held_as=jnp.bfloat16):
    values = jax.random.normal(stream_key, dims, jnp.float32) * spread
    if len(cuts) > 0:
        values = steps_of(stream_key, dims, cuts, -0.22, 0.18) * values
    return jnp.clip(values, min=-most, max=most).astype(held_as)


def setup_inputs(seed: int = 0) -> dict:
    streams_of = jax.random.split(jax.random.key(seed), 8)
    output_gradient = centred(streams_of[0], (TOKENS, MODEL_WIDTH), 1.0, 6.0, ((0, 8), (1, 4)))
    gate_preactivation = centred(streams_of[1], (TOKENS, HIDDEN_SHARE), 1.5, 8.0, ((0, 8), (1, 4)))
    up_preactivation = centred(streams_of[2], (TOKENS, HIDDEN_SHARE), 1.0, 6.0, ((0, 8), (1, 4)))
    down_weight = centred(streams_of[3], (HIDDEN_SHARE, MODEL_WIDTH), HIDDEN_SHARE ** -0.5, 0.0625, ((0, 4),))
    adapter_first = centred(streams_of[4], (HIDDEN_SHARE, ADAPTER_RANK), HIDDEN_SHARE ** -0.5, 0.0625, ((0, 4),))
    adapter_second = centred(streams_of[5], (ADAPTER_RANK, MODEL_WIDTH), MODEL_WIDTH ** -0.5, 0.09375)
    plan = draw_plan(jax.random.fold_in(streams_of[7], 71), 0)
    return dict(output_gradient=output_gradient, gate_preactivation=gate_preactivation, up_preactivation=up_preactivation, down_weight=down_weight, adapter_first=adapter_first, adapter_second=adapter_second, plan=plan)


def reference(output_gradient, gate_preactivation, up_preactivation, down_weight, adapter_first, adapter_second, plan):
    block_count = plan.shape[0]
    owned = block_count // N_DP
    block_index = jnp.arange(block_count, dtype=jnp.int32)
    same_owner = (plan[None, :] == plan[:, None]) & (block_index[None, :] < block_index[:, None])
    rank_in = jnp.sum(same_owner.astype(jnp.int32), axis=1).astype(jnp.int32)
    target = (plan * owned + rank_in).astype(jnp.int32)
    blocks_of = output_gradient.reshape(block_count, -1)
    packed_tokens = jnp.zeros_like(blocks_of).at[target].set(blocks_of).reshape(output_gradient.shape)
    gate_vals = gate_preactivation.astype(jnp.float32)
    up_vals = up_preactivation.astype(jnp.float32)
    sigmoid_gate = jax.nn.sigmoid(gate_vals)
    silu_gate = gate_vals * sigmoid_gate
    hidden_units = (silu_gate * up_vals).astype(jnp.bfloat16)
    low_rank_rows = jnp.dot(hidden_units, adapter_first, preferred_element_type=jnp.float32).astype(jnp.bfloat16)
    passed_through = lax.dot_general(packed_tokens, adapter_second, (((1,), (1,)), ((), ())), preferred_element_type=jnp.float32).astype(jnp.bfloat16)
    hidden_gradient = lax.dot_general(packed_tokens, down_weight, (((1,), (1,)), ((), ())), preferred_element_type=jnp.float32)
    hidden_gradient = hidden_gradient + lax.dot_general(passed_through, adapter_first, (((1,), (1,)), ((), ())), preferred_element_type=jnp.float32)
    grad_gate = (hidden_gradient * up_vals * sigmoid_gate * (1.0 + gate_vals * (1.0 - sigmoid_gate))).astype(jnp.bfloat16)
    grad_up = (hidden_gradient * silu_gate).astype(jnp.bfloat16)
    grad_a = lax.dot_general(hidden_units, passed_through, (((0,), (0,)), ((), ())), preferred_element_type=jnp.float32)
    grad_b = lax.dot_general(low_rank_rows, packed_tokens, (((0,), (0,)), ((), ())), preferred_element_type=jnp.float32)
    return grad_gate, grad_up, grad_a.reshape(N_MP, -1, grad_a.shape[1]), grad_b
```

```python
import functools

import jax
import jax.numpy as jnp
from jax import lax
from jax.experimental import pallas as pl
from jax.experimental.pallas import tpu as pltpu
from jax.sharding import PartitionSpec as P


F32 = jnp.float32
BF16 = jnp.bfloat16
LANES = 128
SUB = 8
NT = (((1,), (1,)), ((), ()))
TN = (((0,), (0,)), ((), ()))


def dot(a, b, dims):
    return lax.dot_general(a, b, dims, preferred_element_type=F32)


def vspec():
    return pl.BlockSpec(memory_space=pltpu.VMEM)


def sspec():
    return pl.BlockSpec(memory_space=pltpu.SMEM)


def call(kernel, out_shape, n_smem, n_vmem, name, flops=0, nbytes=0, scratch=()):
    many = isinstance(out_shape, (list, tuple))
    return pl.pallas_call(
        kernel,
        out_shape=out_shape,
        in_specs=[sspec()] * n_smem + [vspec()] * n_vmem,
        out_specs=[vspec()] * len(out_shape) if many else vspec(),
        scratch_shapes=list(scratch),
        cost_estimate=pl.CostEstimate(flops=flops, bytes_accessed=nbytes, transcendentals=0),
        name=name,
    )


def pack_kernel(capacity, plan_ref, blocks_ref, out_ref, counts):
    owned = blocks_ref.shape[0]
    for owner in range(owned // capacity):
        counts[owner] = 0
    for block in range(owned):
        owner = plan_ref[block]
        rank = counts[owner]
        counts[owner] = rank + 1
        out_ref[owner * capacity + rank] = blocks_ref[block]


def act_kernel(groups, gate_ref, up_ref, first_ref, padded_ref, silu_ref, slope_ref, low_ref, hidden):
    rows, width = gate_ref.shape
    per = width // groups
    step = 16

    def one(index, carry):
        at = pl.ds(pl.multiple_of(index * step, step), step)
        gate = gate_ref[at, :].astype(F32)
        up = up_ref[at, :].astype(F32)
        sig = jax.nn.sigmoid(gate)
        silu = gate * sig
        silu_ref[at, :] = silu
        slope_ref[at, :] = up * sig * (1.0 + gate * (1.0 - sig))
        hidden[at, :] = (silu * up).astype(BF16)
        return carry

    lax.fori_loop(0, rows // step, one, 0)
    low_ref[...] = dot(hidden[...], first_ref[...], NT)
    room = padded_ref.shape[2]
    for group in range(groups):
        padded_ref[group, :, pl.ds(0, per)] = hidden[:, group * per : (group + 1) * per]
        if room > per:
            padded_ref[group, :, pl.ds(per, room - per)] = jnp.zeros((rows, room - per), BF16)


def through_kernel(me_ref, x_ref, second_ref, out_ref):
    width = x_ref.shape[1]
    cols = pl.ds(pl.multiple_of(me_ref[0] * width, LANES), width)
    out_ref[...] = dot(x_ref[...], second_ref[:, cols], NT)


def layout_of(rank, per, brows, width):
    full, rem = per // LANES, per % LANES
    half = 0 < rem <= LANES // 2 and rank % (2 * SUB) == 0
    a_rows = rank * full + (0 if rem == 0 else rank // 2 if half else rank)
    q, r = brows // SUB, brows % SUB
    blocks = width // LANES
    share = SUB // r if r else 1
    b_rows = blocks * q * SUB + (-(-blocks // share) * SUB if r else 0)
    return full, rem, half, a_rows, q, r, blocks, share, b_rows


def make_send(groups, per, brows, width, rank):
    full, rem, half, a_rows, q, r, blocks, share, b_rows = layout_of(rank, per, brows, width)

    def kernel(part_ref, other_ref, padded_ref, low_a_ref, low_b_ref, x_ref, out_ref, through_ref, prod):
        through = (part_ref[...].astype(F32) + other_ref[...].astype(F32)).astype(BF16)
        through_ref[...] = through
        low = (low_a_ref[...] + low_b_ref[...]).astype(BF16)
        prod[...] = dot(low, x_ref[...], TN)
        for group in range(groups):
            piece = dot(through, padded_ref[group], TN)
            for j in range(full):
                out_ref[group, pl.ds(j * rank, rank), :] = piece[:, j * LANES : (j + 1) * LANES].astype(BF16)
            if rem:
                last = piece[:, full * LANES : (full + 1) * LANES]
                if half:
                    last = last[: rank // 2] + pltpu.roll(last[rank // 2 :], LANES // 2, 1)
                out_ref[group, pl.ds(full * rank, last.shape[0]), :] = last.astype(BF16)
            at = a_rows
            base = group * brows
            for j in range(blocks):
                for k in range(q):
                    out_ref[group, pl.ds(at, SUB), :] = prod[
                        pl.ds(base + k * SUB, SUB), pl.ds(j * LANES, LANES)
                    ].astype(BF16)
                    at += SUB
            if r:
                for j in range(0, blocks, share):
                    pieces = [
                        prod[pl.ds(base + q * SUB, r), pl.ds(i * LANES, LANES)] for i in range(j, min(j + share, blocks))
                    ]
                    lack = SUB - r * len(pieces)
                    if lack:
                        pieces.append(jnp.zeros((lack, LANES), F32))
                    out_ref[group, pl.ds(at, SUB), :] = jnp.concatenate(pieces, 0).astype(BF16)
                    at += SUB

    return kernel, a_rows + b_rows


def make_sum(groups, per, brows, width, rank):
    full, rem, half, a_rows, q, r, blocks, share, b_rows = layout_of(rank, per, brows, width)

    def kernel(in_ref, a_ref, b_ref, total):
        acc = in_ref[0].astype(F32)
        for group in range(1, groups):
            acc = acc + in_ref[group].astype(F32)
        total[...] = acc
        for j in range(full):
            a_ref[0, :, pl.ds(j * LANES, LANES)] = total[pl.ds(j * rank, rank), :]
        if rem:
            if half:
                last = total[pl.ds(full * rank, rank // 2), :]
                a_ref[0, pl.ds(0, rank // 2), pl.ds(full * LANES, rem)] = last[:, :rem]
                a_ref[0, pl.ds(rank // 2, rank // 2), pl.ds(full * LANES, rem)] = pltpu.roll(last, LANES // 2, 1)[:, :rem]
            else:
                a_ref[0, :, pl.ds(full * LANES, rem)] = total[pl.ds(full * rank, rank), :][:, :rem]
        at = a_rows
        for j in range(blocks):
            for k in range(q):
                b_ref[pl.ds(k * SUB, SUB), pl.ds(j * LANES, LANES)] = total[pl.ds(at, SUB), :]
                at += SUB
        if r:
            for j in range(0, blocks, share):
                for i in range(j, min(j + share, blocks)):
                    b_ref[pl.ds(q * SUB, r), pl.ds(i * LANES, LANES)] = total[pl.ds(at + (i - j) * r, r), :]
                at += SUB

    return kernel


def join_kernel(me_ref, own_ref, core_ref, x_ref, far_ref, out_ref):
    width = own_ref.shape[1]
    for bit, ref in enumerate((own_ref, core_ref, x_ref, far_ref)):
        cols = pl.ds(pl.multiple_of((me_ref[0] ^ bit) * width, LANES), width)
        out_ref[:, cols] = ref[...]


def main_kernel(me_ref, own_ref, core_ref, x_ref, far_ref, through_ref, first_ref, weight_ref, silu_ref, slope_ref, gate_ref, up_ref):
    width = own_ref.shape[1]
    acc = dot(through_ref[...], first_ref[...], (((1,), (0,)), ((), ())))
    for bit, ref in enumerate((own_ref, core_ref, x_ref, far_ref)):
        cols = pl.ds(pl.multiple_of((me_ref[0] ^ bit) * width, LANES), width)
        acc = acc + dot(ref[...], weight_ref[:, cols], NT)
    gate_ref[...] = (acc * slope_ref[...]).astype(BF16)
    up_ref[...] = (acc * silu_ref[...]).astype(BF16)


def main_call(me, own, core, other, far, through, first_t, weight, silu, slope, tile=256):
    rows, width = own.shape
    hid, model = weight.shape
    rank = through.shape[1]
    steps = -(-hid // tile)
    whole = lambda shape: pl.BlockSpec(shape, lambda i, me: (0, 0))
    block = pl.BlockSpec((rows, tile), lambda i, me: (0, i))
    return pl.pallas_call(
        main_kernel,
        out_shape=[jax.ShapeDtypeStruct((rows, hid), BF16)] * 2,
        grid_spec=pltpu.PrefetchScalarGridSpec(
            num_scalar_prefetch=1,
            grid=(steps,),
            in_specs=[whole((rows, width))] * 4
            + [whole((rows, rank)), pl.BlockSpec((rank, tile), lambda i, me: (0, i)), pl.BlockSpec((tile, model), lambda i, me: (i, 0)), block, block],
            out_specs=[block, block],
        ),
        cost_estimate=pl.CostEstimate(flops=2 * rows * hid * model, bytes_accessed=2 * hid * model, transcendentals=0),
        name="main",
    )(me, own, core, other, far, through, first_t, weight, silu, slope)


def swap(value, bit):
    count = lax.axis_size("mp")
    return lax.ppermute(value, "mp", [(i, i ^ bit) for i in range(count)])


def fast_body(output_gradient, gate_preactivation, up_preactivation, down_weight, adapter_first, adapter_second, plan):
    groups = lax.axis_size("dp")
    owned = plan.shape[0]
    capacity = owned // groups
    tokens, width = output_gradient.shape
    hid, rank = adapter_first.shape
    per, brows = hid // groups, rank // groups
    tall = tokens // owned
    me = lax.axis_index("mp").astype(jnp.int32).reshape(1)
    first_t = adapter_first.T

    outgoing = call(
        functools.partial(pack_kernel, capacity),
        jax.ShapeDtypeStruct((owned, tall, width), BF16),
        1,
        1,
        "pack",
        nbytes=4 * tokens * width,
        scratch=[pltpu.SMEM((groups,), jnp.int32)],
    )(plan, output_gradient.reshape(owned, tall, width))
    packed = lax.all_to_all(outgoing, "dp", split_axis=0, concat_axis=0, tiled=True).reshape(tokens, width)

    room = -(-per // LANES) * LANES
    padded, silu, slope, low_part = call(
        functools.partial(act_kernel, groups),
        [
            jax.ShapeDtypeStruct((groups, tokens, room), BF16),
            jax.ShapeDtypeStruct((tokens, hid), F32),
            jax.ShapeDtypeStruct((tokens, hid), F32),
            jax.ShapeDtypeStruct((tokens, rank), F32),
        ],
        0,
        3,
        "act",
        flops=2 * tokens * hid * rank,
        nbytes=tokens * hid * 14,
        scratch=[pltpu.VMEM((tokens, hid), BF16)],
    )(gate_preactivation, up_preactivation, first_t)
    low_a = low_part + swap(low_part, 1)
    low_b = swap(low_a, 2)

    through_part = call(
        through_kernel,
        jax.ShapeDtypeStruct((tokens, rank), F32),
        1,
        2,
        "through",
        flops=2 * tokens * width * rank,
        nbytes=2 * tokens * width,
    )(me, packed, adapter_second)
    half_a = (through_part + swap(through_part, 1)).astype(BF16)
    half_b = swap(half_a, 2)

    side = swap(packed, 2)
    core = swap(packed, 1)
    far = swap(side, 1)

    send, rows_sent = make_send(groups, per, brows, width, rank)
    payload, through = call(
        send,
        [jax.ShapeDtypeStruct((groups, rows_sent, LANES), BF16), jax.ShapeDtypeStruct((tokens, rank), BF16)],
        0,
        6,
        "send",
        flops=2 * tokens * hid * rank,
        nbytes=tokens * hid * 2,
        scratch=[pltpu.VMEM((rank, width), F32)],
    )(half_a, half_b, padded, low_a, low_b, packed)
    landed = lax.all_to_all(payload, "dp", split_axis=0, concat_axis=0, tiled=True)

    grad_gate, grad_up = main_call(me, packed, core, side, far, through, first_t, down_weight, silu, slope)

    grad_a_t, part_b = call(
        make_sum(groups, per, brows, width, rank),
        [jax.ShapeDtypeStruct((1, rank, per), F32), jax.ShapeDtypeStruct((brows, width), F32)],
        0,
        1,
        "sum",
        nbytes=2 * groups * rows_sent * LANES,
        scratch=[pltpu.VMEM((rows_sent, LANES), F32)],
    )(landed)
    grad_b = call(
        join_kernel,
        jax.ShapeDtypeStruct((brows, 4 * width), F32),
        1,
        4,
        "join",
        nbytes=32 * brows * width,
    )(me, part_b, swap(part_b, 1), swap(part_b, 2), swap(part_b, 3))
    return grad_gate, grad_up, jnp.swapaxes(grad_a_t, 1, 2), grad_b


def general_body(
    output_gradient,
    gate_preactivation,
    up_preactivation,
    down_weight,
    adapter_first,
    adapter_second,
    plan,
):
    groups = lax.axis_size("dp")
    owned = plan.shape[0]
    capacity = -(-owned // groups)
    tokens_here = output_gradient.shape[0]
    feature_cols = output_gradient.shape[1]
    block_width = tokens_here // owned * feature_cols
    slot_count = groups * capacity
    positions = jnp.arange(owned, dtype=jnp.int32)
    earlier = (plan[None, :] == plan[:, None]) & (positions[None, :] < positions[:, None])
    target = plan * capacity + jnp.sum(earlier.astype(jnp.int32), axis=1)
    sending = target[None, :] == jnp.arange(slot_count, dtype=jnp.int32)[:, None]
    outgoing = jnp.dot(
        sending.astype(jnp.bfloat16),
        output_gradient.reshape(owned, block_width),
        preferred_element_type=jnp.float32,
    ).astype(jnp.bfloat16)
    filled = jnp.sum(sending.astype(jnp.float32), axis=1).astype(jnp.bfloat16)
    arrived, present = (
        lax.all_to_all(outgoing, "dp", split_axis=0, concat_axis=0, tiled=True),
        lax.all_to_all(filled, "dp", split_axis=0, concat_axis=0, tiled=True),
    )
    present_flag = present.astype(jnp.int32)
    ranking = jnp.cumsum(present_flag) - 1
    keeping = (ranking[None, :] == positions[:, None]) & (present_flag[None, :] > 0)
    packed_tokens = (
        jnp.dot(keeping.astype(jnp.bfloat16), arrived, preferred_element_type=jnp.float32)
        .astype(jnp.bfloat16)
        .reshape(tokens_here, feature_cols)
    )
    feature_rows = lax.all_gather(packed_tokens, "mp", axis=1, tiled=True)
    gate_vals = gate_preactivation.astype(jnp.float32)
    up_vals = up_preactivation.astype(jnp.float32)
    sigmoid_gate = jax.nn.sigmoid(gate_vals)
    silu_gate = gate_vals * sigmoid_gate
    hidden_units = (silu_gate * up_vals).astype(jnp.bfloat16)
    low_rank_piece = jnp.dot(hidden_units, adapter_first, preferred_element_type=jnp.float32)
    low_rank_rows = lax.psum(low_rank_piece, "mp").astype(jnp.bfloat16)
    passed_through = lax.dot_general(
        feature_rows, adapter_second, (((1,), (1,)), ((), ())), preferred_element_type=jnp.float32
    ).astype(jnp.bfloat16)
    grad_a_rows = lax.psum_scatter(
        lax.dot_general(
            hidden_units,
            passed_through,
            (((0,), (0,)), ((), ())),
            preferred_element_type=jnp.float32,
        ),
        "dp",
        scatter_dimension=0,
        tiled=True,
    )
    part_rows = lax.psum_scatter(
        lax.dot_general(
            low_rank_rows,
            packed_tokens,
            (((0,), (0,)), ((), ())),
            preferred_element_type=jnp.float32,
        ),
        "dp",
        scatter_dimension=0,
        tiled=True,
    )
    grad_b_rows = lax.all_gather(part_rows, "mp", axis=1, tiled=True)
    hidden_gradient = lax.dot_general(
        feature_rows, down_weight, (((1,), (1,)), ((), ())), preferred_element_type=jnp.float32
    )
    hidden_gradient = hidden_gradient + lax.dot_general(
        passed_through, adapter_first, (((1,), (1,)), ((), ())), preferred_element_type=jnp.float32
    )
    grad_gate = (
        hidden_gradient * up_vals * sigmoid_gate * (1.0 + gate_vals * (1.0 - sigmoid_gate))
    ).astype(jnp.bfloat16)
    grad_up = (hidden_gradient * silu_gate).astype(jnp.bfloat16)
    return (grad_gate, grad_up, grad_a_rows[None], grad_b_rows)


def fits(mesh, args):
    groups, parts = mesh.shape["dp"], mesh.shape["mp"]
    gradient, gate, _, weight, first, second, plan = args
    owned = plan.shape[0] // groups
    tokens, width = gradient.shape[0] // groups, gradient.shape[1] // parts
    hid, rank = first.shape[0] // parts, first.shape[1]
    return (
        parts == 4
        and owned % groups == 0
        and tokens == owned * SUB
        and tokens % 16 == 0
        and width % LANES == 0
        and hid % groups == 0
        and rank % groups == 0
        and rank % (2 * SUB) == 0
        and SUB % max(rank // groups % SUB, 1) == 0
    )


def solution(mesh):
    def step(*args):
        return jax.shard_map(
            fast_body if fits(mesh, args) else general_body,
            mesh=mesh,
            in_specs=(
                P("dp", "mp"),
                P("dp", "mp"),
                P("dp", "mp"),
                P("mp", None),
                P("mp", None),
                P(),
                P("dp"),
            ),
            out_specs=(P("dp", "mp"), P("dp", "mp"), P("mp", "dp", None), P("dp", None)),
            check_vma=False,
        )(*args)

    return step
```

```python
import functools

import jax
import jax.numpy as jnp
from jax import lax
from jax.experimental import pallas as pl
from jax.experimental.pallas import tpu as pltpu
from jax.sharding import PartitionSpec as P


F32 = jnp.float32
BF16 = jnp.bfloat16
LANES = 128
SUB = 8
NT = (((1,), (1,)), ((), ()))
TN = (((0,), (0,)), ((), ()))


def dot(a, b, dims):
    return lax.dot_general(a, b, dims, preferred_element_type=F32)


def sspec():
    return pl.BlockSpec(memory_space=pltpu.SMEM)


def layout_of(rank, per, brows, width):
    full, rem = per // LANES, per % LANES
    half = 0 < rem <= LANES // 2 and rank % (2 * SUB) == 0
    a_rows = rank * full + (0 if rem == 0 else rank // 2 if half else rank)
    q, r = brows // SUB, brows % SUB
    blocks = width // LANES
    share = SUB // r if r else 1
    b_rows = blocks * q * SUB + (-(-blocks // share) * SUB if r else 0)
    return full, rem, half, a_rows, q, r, blocks, share, b_rows


ON_CHIP_KIB = 65472
ROOM = 12500


def full(array):
    zeros = (0,) * len(array.shape)
    return pl.BlockSpec(array.shape, lambda: zeros)


def far_off():
    return pl.BlockSpec(memory_space=pltpu.HBM)


def call(kernel, outs, smem=(), hbm=(), args=(), flops=0, scratch=(), room=48000, hbm_outs=0):
    nbytes = sum(a.size * a.dtype.itemsize for a in (*hbm, *args, *outs))
    got = pl.pallas_call(
        kernel,
        out_shape=list(outs),
        in_specs=[sspec() for _ in smem] + [far_off() for _ in hbm] + [full(a) for a in args],
        out_specs=[far_off() if at < hbm_outs else full(a) for at, a in enumerate(outs)],
        scratch_shapes=list(scratch),
        cost_estimate=pl.CostEstimate(flops=flops, bytes_accessed=nbytes, transcendentals=0),
        compiler_params=pltpu.CompilerParams(vmem_limit_bytes=(ON_CHIP_KIB - room) * 2**10),
    )(*smem, *hbm, *args)
    return got[0] if len(outs) == 1 else got


def fetch(pairs, sems):
    copies = [pltpu.make_async_copy(a, b, sems.at[i]) for i, (a, b) in enumerate(pairs)]
    for copy in copies:
        copy.start()
    return copies


def pack_kernel(capacity, plan_ref, blocks_ref, out_ref, blocks, plan, counts, sems):
    owned = blocks_ref.shape[0]
    loads = fetch([(plan_ref, plan), (blocks_ref, blocks)], sems)
    for owner in range(owned // capacity):
        counts[owner] = 0
    for load in loads:
        load.wait()
    copies = []
    for block in range(owned):
        owner = plan[block]
        rank = counts[owner]
        counts[owner] = rank + 1
        copies += fetch([(blocks.at[block], out_ref.at[owner * capacity + rank])], sems.at[pl.ds(2 + block, 1)])
    for copy in copies:
        copy.wait()


def act_kernel(groups, me_ref, gate_ref, up_ref, first_ref, second_ref, padded_ref, low_ref, mine_ref, hidden):
    rows, width = gate_ref.shape
    per = width // groups
    step = 16
    mine_ref[...] = second_ref[:, columns(me_ref, 0, mine_ref.shape[1])]

    def one(index, carry):
        at = pl.ds(pl.multiple_of(index * step, step), step)
        gate_vals = gate_ref[at, :].astype(F32)
        silu = gate_vals * jax.nn.sigmoid(gate_vals)
        hidden[at, :] = (silu * up_ref[at, :].astype(F32)).astype(BF16)
        return carry

    lax.fori_loop(0, rows // step, one, 0)
    room = padded_ref.shape[2]
    for group in range(groups):
        padded_ref[group, :, pl.ds(0, per)] = hidden[:, group * per : (group + 1) * per]
        if room > per:
            padded_ref[group, :, pl.ds(per, room - per)] = jnp.zeros((rows, room - per), BF16)
    low_ref[...] = dot(hidden[...], first_ref[...], NT)


def shaped(shape, dtype):
    return jax.ShapeDtypeStruct(shape, dtype)


def columns(me, bit, width):
    return pl.ds(pl.multiple_of((me[0] ^ bit) * width, LANES), width)


def through_kernel(own_ref, second_ref, out_ref):
    out_ref[...] = dot(own_ref[...], second_ref[...], NT).astype(BF16)


def add_kernel(one_ref, other_ref, out_ref):
    out_ref[...] = one_ref[...] + other_ref[...]


def make_share(groups, brows, width, rank, per):
    _, _, _, _, q, r, blocks, share, _ = layout_of(rank, per, brows, width)

    def kernel(here_ref, x_ref, low_a, low_b, out_ref, prod):
        low = (low_a[...] + low_b[...]).astype(BF16)
        prod[...] = dot(low, x_ref[...], TN)
        for group in range(groups):
            at = 0
            for j in range(blocks):
                for k in range(q):
                    out_ref[group, pl.ds(at, SUB), :] = prod[
                        pl.ds(group * brows + k * SUB, SUB), pl.ds(j * LANES, LANES)
                    ].astype(BF16)
                    at += SUB
            if r:
                for j in range(0, blocks, share):
                    pieces = [
                        prod[pl.ds(group * brows + q * SUB, r), pl.ds(i * LANES, LANES)]
                        for i in range(j, min(j + share, blocks))
                    ]
                    lack = SUB - r * len(pieces)
                    if lack:
                        pieces.append(jnp.zeros((lack, LANES), F32))
                    out_ref[group, pl.ds(at, SUB), :] = jnp.concatenate(pieces, 0).astype(BF16)
                    at += SUB

    return kernel


def make_send(groups, brows, width, rank, per):
    full_, rem, half, a_rows, _, _, _, _, b_rows = layout_of(rank, per, brows, width)

    def kernel(here_ref, part_0, part_1, part_2, part_3, padded_ref, share_ref, through_ref, *outs):
        parts = [part[...].astype(F32) for part in (part_0, part_1, part_2, part_3)]
        through = ((parts[0] + parts[1]) + (parts[2] + parts[3])).astype(BF16)
        through_ref[...] = through
        for peer, out_ref in enumerate(outs):
            for side in range(2):
                group = here_ref[0] ^ (peer + side * len(outs))
                piece = dot(through, padded_ref[group], TN)
                for j in range(full_):
                    out_ref[side, pl.ds(j * rank, rank), :] = piece[:, j * LANES : (j + 1) * LANES].astype(BF16)
                if rem:
                    last = piece[:, full_ * LANES : (full_ + 1) * LANES]
                    if half:
                        last = last[: rank // 2] + pltpu.roll(last[rank // 2 :], LANES // 2, 1)
                    out_ref[side, pl.ds(full_ * rank, last.shape[0]), :] = last.astype(BF16)
                out_ref[side, pl.ds(a_rows, b_rows), :] = share_ref[group]

    return kernel


def half_kernel(*refs):
    *parts, mine_ref, other_ref = refs
    for side in range(2):
        total = parts[0][side].astype(F32)
        for part in parts[1:]:
            total = total + part[side].astype(F32)
        if side:
            other_ref[...] = total.astype(BF16)
        else:
            mine_ref[...] = total


def make_sum_b(groups, brows, width, rank, per):
    _, _, _, a_rows, _, _, _, _, b_rows = layout_of(rank, per, brows, width)

    def kernel(mine_ref, other_ref, out_ref):
        at = pl.ds(a_rows, b_rows)
        out_ref[...] = mine_ref[at] + other_ref[at].astype(F32)

    return kernel


def make_sum_a(groups, brows, width, rank, per):
    full_, rem, half, a_rows, *_ = layout_of(rank, per, brows, width)

    def kernel(mine_ref, other_ref, a_ref, total):
        at = pl.ds(0, a_rows)
        total[...] = mine_ref[at] + other_ref[at].astype(F32)
        for j in range(full_):
            a_ref[0, :, pl.ds(j * LANES, LANES)] = total[pl.ds(j * rank, rank), :]
        if rem:
            at = pl.ds(full_ * LANES, rem)
            if half:
                last = total[pl.ds(full_ * rank, rank // 2), :]
                a_ref[0, pl.ds(0, rank // 2), at] = last[:, :rem]
                a_ref[0, pl.ds(rank // 2, rank // 2), at] = pltpu.roll(last, LANES // 2, 1)[:, :rem]
            else:
                a_ref[0, :, at] = total[pl.ds(full_ * rank, rank), :][:, :rem]

    return kernel


def make_join(groups, brows, width, rank, per):
    _, _, _, _, q, r, blocks, share, _ = layout_of(rank, per, brows, width)

    def kernel(me_ref, own_ref, core_ref, x_ref, far_ref, out_ref):
        for bit, ref in enumerate((own_ref, core_ref, x_ref, far_ref)):
            base = (me_ref[0] ^ bit) * width
            at = 0
            for j in range(blocks):
                cols = pl.ds(pl.multiple_of(base + j * LANES, LANES), LANES)
                for k in range(q):
                    out_ref[pl.ds(k * SUB, SUB), cols] = ref[pl.ds(at, SUB), :]
                    at += SUB
            if r:
                for j in range(0, blocks, share):
                    for i in range(j, min(j + share, blocks)):
                        cols = pl.ds(pl.multiple_of(base + i * LANES, LANES), LANES)
                        out_ref[pl.ds(q * SUB, r), cols] = ref[pl.ds(at + (i - j) * r, r), :]
                    at += SUB

    return kernel


def near_kernel(
    tile, me_ref, first_ref, weight_ref, own_ref, core_ref, through_ref, out_ref, first, weight, total, arrive, leave
):
    hid = weight_ref.shape[0]
    width = own_ref.shape[1]
    spans = [pl.ds(at, min(tile, hid - at)) for at in range(0, hid, tile)]
    coming = fetch([(weight_ref.at[:, columns(me_ref, bit, width)], weight.at[bit]) for bit in range(2)], arrive)
    small = fetch([(first_ref, first)], arrive.at[pl.ds(2, 1)])
    small[0].wait()
    for span in spans:
        total[:, span] = dot(through_ref[...], first[:, span], (((1,), (0,)), ((), ())))
    leaving = []
    for bit, ref in enumerate((own_ref, core_ref)):
        coming[bit].wait()
        for index, span in enumerate(spans):
            total[:, span] += dot(ref[...], weight[bit, span], NT)
            if bit:
                leaving += fetch([(total.at[:, span], out_ref.at[:, span])], leave.at[pl.ds(index, 1)])
    for copy in leaving:
        copy.wait()


def distant_kernel(
    tile, me_ref, weight_ref, total_ref, gate_in, up_in, x_ref, far_ref, gate_ref, up_ref,
    weight, total, gate, up, grad_gate, grad_up, arrive, leave,
):
    hid = weight_ref.shape[0]
    width = x_ref.shape[1]
    spans = [pl.ds(at, min(tile, hid - at)) for at in range(0, hid, tile)]
    coming = fetch(
        [
            (weight_ref.at[:, columns(me_ref, 2, width)], weight.at[0]),
            (total_ref, total),
            (weight_ref.at[:, columns(me_ref, 3, width)], weight.at[1]),
            (gate_in, gate),
            (up_in, up),
        ],
        arrive,
    )
    leaving = []
    coming[0].wait()
    coming[1].wait()
    for span in spans:
        total[:, span] += dot(x_ref[...], weight[0, span], NT)
    for copy in coming[2:]:
        copy.wait()
    for index, span in enumerate(spans):
        acc = total[:, span] + dot(far_ref[...], weight[1, span], NT)
        gate_vals = gate[:, span].astype(F32)
        sig = jax.nn.sigmoid(gate_vals)
        slope = up[:, span].astype(F32) * sig * (1.0 + gate_vals * (1.0 - sig))
        grad_gate[:, span] = (acc * slope).astype(BF16)
        grad_up[:, span] = (acc * (gate_vals * sig)).astype(BF16)
        leaving += fetch([(grad_gate.at[:, span], gate_ref.at[:, span]), (grad_up.at[:, span], up_ref.at[:, span])], leave.at[index])
    for copy in leaving:
        copy.wait()


def near_call(me, own, core, through, first_t, weight, tile=512):
    rows, width = own.shape
    hid = weight.shape[0]
    rank = through.shape[1]
    return call(
        functools.partial(near_kernel, tile),
        [shaped((rows, hid), F32)],
        [me],
        [first_t, weight],
        [own, core, through],
        flops=4 * rows * hid * width,
        scratch=[
            pltpu.VMEM((rank, hid), BF16),
            pltpu.VMEM((2, hid, width), BF16),
            pltpu.VMEM((rows, hid), F32),
            pltpu.SemaphoreType.DMA((3,)),
            pltpu.SemaphoreType.DMA((-(-hid // tile),)),
        ],
        room=ROOM,
        hbm_outs=1,
    )


def distant_call(me, total, other, far, weight, gate, up, tile=512):
    rows, width = other.shape
    hid = weight.shape[0]
    return call(
        functools.partial(distant_kernel, tile),
        [shaped((rows, hid), BF16)] * 2,
        [me],
        [weight, total, gate, up],
        [other, far],
        flops=4 * rows * hid * width,
        scratch=[
            pltpu.VMEM((2, hid, width), BF16),
            pltpu.VMEM((rows, hid), F32),
            *[pltpu.VMEM((rows, hid), BF16)] * 4,
            pltpu.SemaphoreType.DMA((5,)),
            pltpu.SemaphoreType.DMA((-(-hid // tile), 2)),
        ],
        room=ROOM,
        hbm_outs=2,
    )


def swap(value, bit):
    count = lax.axis_size("mp")
    return lax.ppermute(value, "mp", [(i, i ^ bit) for i in range(count)])


def trade(value, bit):
    count = lax.axis_size("dp")
    return lax.ppermute(value, "dp", [(i, i ^ bit) for i in range(count)])


def fast_body(*args):
    return fast_layer(*args)


def fast_layer(output_gradient, gate_preactivation, up_preactivation, down_weight, adapter_first, adapter_second, plan):
    groups = lax.axis_size("dp")
    owned = plan.shape[0]
    capacity = owned // groups
    tokens, width = output_gradient.shape
    hid, rank = adapter_first.shape
    per, brows = hid // groups, rank // groups
    tall = tokens // owned
    me = lax.axis_index("mp").astype(jnp.int32).reshape(1)
    here = lax.axis_index("dp").astype(jnp.int32).reshape(1)
    first_t = adapter_first.T
    room = -(-per // LANES) * LANES
    _, _, _, a_rows, _, _, _, _, b_rows = layout_of(rank, per, brows, width)
    sizes = (groups, brows, width, rank, per)

    outgoing = call(
        functools.partial(pack_kernel, capacity),
        [shaped((owned, tall, width), BF16)],
        hbm=[plan, output_gradient.reshape(owned, tall, width)],
        scratch=[
            pltpu.VMEM((owned, tall, width), BF16),
            pltpu.SMEM((owned,), jnp.int32),
            pltpu.SMEM((groups,), jnp.int32),
            pltpu.SemaphoreType.DMA((owned + 2,)),
        ],
        room=0,
        hbm_outs=1,
    )
    packed = lax.all_to_all(outgoing, "dp", split_axis=0, concat_axis=0, tiled=True).reshape(tokens, width)

    padded, low_0, second = call(
        functools.partial(act_kernel, groups),
        [
            shaped((groups, tokens, room), BF16),
            shaped((tokens, rank), F32),
            shaped((rank, width), BF16),
        ],
        [me],
        args=[gate_preactivation, up_preactivation, first_t, adapter_second],
        flops=2 * tokens * hid * rank,
        scratch=[pltpu.VMEM((tokens, hid), BF16)],
    )
    low_1 = swap(low_0, 1)
    low_a = call(add_kernel, [shaped((tokens, rank), F32)], args=[low_0, low_1])
    low_b = swap(low_a, 2)

    part_0 = call(
        through_kernel, [shaped((tokens, rank), BF16)], args=[packed, second], flops=2 * tokens * width * rank
    )
    part_2 = swap(part_0, 2)
    part_3 = swap(part_0, 3)
    part_1 = swap(part_0, 1)
    share = call(
        make_share(*sizes),
        [shaped((groups, b_rows, LANES), BF16)],
        [here],
        args=[packed, low_a, low_b],
        scratch=[pltpu.VMEM((rank, width), F32)],
    )
    side = swap(packed, 2)
    core = swap(packed, 1)

    peers = groups // 2
    through, *payload = call(
        make_send(*sizes),
        [shaped((tokens, rank), BF16)] + [shaped((2, a_rows + b_rows, LANES), BF16)] * peers,
        [here],
        args=[part_0, part_1, part_2, part_3, padded, share],
        flops=2 * tokens * hid * rank,
    )
    arrived = [payload[0]]
    for peer in range(1, peers):
        arrived.append(trade(payload[peer], peer))

    total = near_call(me, packed, core, through, first_t, down_weight)
    far = swap(side, 1)
    mine, other = call(
        half_kernel, [shaped((a_rows + b_rows, LANES), F32), shaped((a_rows + b_rows, LANES), BF16)], args=arrived
    )
    landed = trade(other, peers)
    grad_gate, grad_up = distant_call(me, total, side, far, down_weight, gate_preactivation, up_preactivation)

    b_0 = call(make_sum_b(*sizes), [shaped((b_rows, LANES), F32)], args=[mine, landed])
    b_3 = swap(b_0, 3)
    b_2 = swap(b_0, 2)
    b_1 = swap(b_0, 1)
    grad_a_t = call(
        make_sum_a(*sizes),
        [shaped((1, rank, per), F32)],
        args=[mine, landed],
        scratch=[pltpu.VMEM((a_rows, LANES), F32)],
    )
    grad_b = call(make_join(*sizes), [shaped((brows, 4 * width), F32)], [me], args=[b_0, b_1, b_2, b_3])
    return grad_gate, grad_up, jnp.swapaxes(grad_a_t, 1, 2), grad_b


def general_body(
    output_gradient,
    gate_preactivation,
    up_preactivation,
    down_weight,
    adapter_first,
    adapter_second,
    plan,
):
    groups = lax.axis_size("dp")
    owned = plan.shape[0]
    capacity = -(-owned // groups)
    tokens_here = output_gradient.shape[0]
    feature_cols = output_gradient.shape[1]
    block_width = tokens_here // owned * feature_cols
    slot_count = groups * capacity
    positions = jnp.arange(owned, dtype=jnp.int32)
    earlier = (plan[None, :] == plan[:, None]) & (positions[None, :] < positions[:, None])
    target = plan * capacity + jnp.sum(earlier.astype(jnp.int32), axis=1)
    sending = target[None, :] == jnp.arange(slot_count, dtype=jnp.int32)[:, None]
    outgoing = jnp.dot(
        sending.astype(jnp.bfloat16),
        output_gradient.reshape(owned, block_width),
        preferred_element_type=jnp.float32,
    ).astype(jnp.bfloat16)
    filled = jnp.sum(sending.astype(jnp.float32), axis=1).astype(jnp.bfloat16)
    arrived, present = (
        lax.all_to_all(outgoing, "dp", split_axis=0, concat_axis=0, tiled=True),
        lax.all_to_all(filled, "dp", split_axis=0, concat_axis=0, tiled=True),
    )
    present_flag = present.astype(jnp.int32)
    ranking = jnp.cumsum(present_flag) - 1
    keeping = (ranking[None, :] == positions[:, None]) & (present_flag[None, :] > 0)
    packed_tokens = (
        jnp.dot(keeping.astype(jnp.bfloat16), arrived, preferred_element_type=jnp.float32)
        .astype(jnp.bfloat16)
        .reshape(tokens_here, feature_cols)
    )
    feature_rows = lax.all_gather(packed_tokens, "mp", axis=1, tiled=True)
    gate_vals = gate_preactivation.astype(jnp.float32)
    up_vals = up_preactivation.astype(jnp.float32)
    sigmoid_gate = jax.nn.sigmoid(gate_vals)
    silu_gate = gate_vals * sigmoid_gate
    hidden_units = (silu_gate * up_vals).astype(jnp.bfloat16)
    low_rank_piece = jnp.dot(hidden_units, adapter_first, preferred_element_type=jnp.float32)
    low_rank_rows = lax.psum(low_rank_piece, "mp").astype(jnp.bfloat16)
    passed_through = lax.dot_general(
        feature_rows, adapter_second, (((1,), (1,)), ((), ())), preferred_element_type=jnp.float32
    ).astype(jnp.bfloat16)
    grad_a_rows = lax.psum_scatter(
        lax.dot_general(
            hidden_units,
            passed_through,
            (((0,), (0,)), ((), ())),
            preferred_element_type=jnp.float32,
        ),
        "dp",
        scatter_dimension=0,
        tiled=True,
    )
    part_rows = lax.psum_scatter(
        lax.dot_general(
            low_rank_rows,
            packed_tokens,
            (((0,), (0,)), ((), ())),
            preferred_element_type=jnp.float32,
        ),
        "dp",
        scatter_dimension=0,
        tiled=True,
    )
    grad_b_rows = lax.all_gather(part_rows, "mp", axis=1, tiled=True)
    hidden_gradient = lax.dot_general(
        feature_rows, down_weight, (((1,), (1,)), ((), ())), preferred_element_type=jnp.float32
    )
    hidden_gradient = hidden_gradient + lax.dot_general(
        passed_through, adapter_first, (((1,), (1,)), ((), ())), preferred_element_type=jnp.float32
    )
    grad_gate = (
        hidden_gradient * up_vals * sigmoid_gate * (1.0 + gate_vals * (1.0 - sigmoid_gate))
    ).astype(jnp.bfloat16)
    grad_up = (hidden_gradient * silu_gate).astype(jnp.bfloat16)
    return (grad_gate, grad_up, grad_a_rows[None], grad_b_rows)


def fits(mesh, args):
    groups, parts = mesh.shape["dp"], mesh.shape["mp"]
    gradient, _, _, _, first, _, plan = args
    owned = plan.shape[0] // groups
    tokens, width = gradient.shape[0] // groups, gradient.shape[1] // parts
    hid, rank = first.shape[0] // parts, first.shape[1]
    return (
        parts == 4
        and groups > 4 and groups & (groups - 1) == 0
        and owned % groups == 0
        and tokens == owned * SUB
        and tokens % 16 == 0
        and width % LANES == 0
        and hid % groups == 0
        and rank % groups == 0
        and rank % (2 * SUB) == 0
        and SUB % max(rank // groups % SUB, 1) == 0
    )


def solution(mesh):
    def step(*args):
        fast = fits(mesh, args)
        run = jax.shard_map(
            fast_body if fast else general_body,
            mesh=mesh,
            in_specs=(
                P("dp", "mp"),
                P("dp", "mp"),
                P("dp", "mp"),
                P("mp", None),
                P("mp", None),
                P(),
                P("dp"),
            ),
            out_specs=(P("dp", "mp"), P("dp", "mp"), P("mp", "dp", None), P("dp", None)),
            check_vma=False,
        )
        return run(*args)

    return step
```

```python
import functools

import jax
import jax.numpy as jnp
from jax import lax
from jax.experimental import pallas as pl
from jax.experimental.pallas import tpu as pltpu
from jax.sharding import PartitionSpec as P


F32 = jnp.float32
BF16 = jnp.bfloat16
LANES = 128
SUB = 8
NT = (((1,), (1,)), ((), ()))
TN = (((0,), (0,)), ((), ()))


def dot(a, b, dims):
    return lax.dot_general(a, b, dims, preferred_element_type=F32)


def sspec():
    return pl.BlockSpec(memory_space=pltpu.SMEM)


def layout_of(rank, per, brows, width):
    full, rem = per // LANES, per % LANES
    half = 0 < rem <= LANES // 2 and rank % (2 * SUB) == 0
    a_rows = rank * full + (0 if rem == 0 else rank // 2 if half else rank)
    q, r = brows // SUB, brows % SUB
    blocks = width // LANES
    share = SUB // r if r else 1
    b_rows = blocks * q * SUB + (-(-blocks // share) * SUB if r else 0)
    return full, rem, half, a_rows, q, r, blocks, share, b_rows


ON_CHIP_KIB = 65472
ROOM = 12500


def full(array):
    zeros = (0,) * len(array.shape)
    return pl.BlockSpec(array.shape, lambda: zeros)


def far_off():
    return pl.BlockSpec(memory_space=pl.ANY)


def call(kernel, outs, smem=(), hbm=(), args=(), flops=0, scratch=(), room=48000, hbm_outs=0):
    nbytes = sum(a.size * a.dtype.itemsize for a in (*hbm, *args, *outs))
    got = pl.pallas_call(
        kernel,
        out_shape=list(outs),
        in_specs=[sspec() for _ in smem] + [far_off() for _ in hbm] + [full(a) for a in args],
        out_specs=[far_off() if at < hbm_outs else full(a) for at, a in enumerate(outs)],
        scratch_shapes=list(scratch),
        cost_estimate=pl.CostEstimate(flops=flops, bytes_accessed=nbytes, transcendentals=0),
        compiler_params=pltpu.CompilerParams(vmem_limit_bytes=(ON_CHIP_KIB - room) * 2**10),
    )(*smem, *hbm, *args)
    return got[0] if len(outs) == 1 else got


def fetch(pairs, sems):
    copies = [pltpu.make_async_copy(a, b, sems.at[i]) for i, (a, b) in enumerate(pairs)]
    for copy in copies:
        copy.start()
    return copies


def pack_kernel(capacity, plan_ref, blocks_ref, out_ref, blocks, plan, counts, sems):
    owned = blocks_ref.shape[0]
    loads = fetch([(plan_ref, plan), (blocks_ref, blocks)], sems)
    for owner in range(owned // capacity):
        counts[owner] = 0
    for load in loads:
        load.wait()
    copies = []
    for block in range(owned):
        owner = plan[block]
        rank = counts[owner]
        counts[owner] = rank + 1
        copies += fetch([(blocks.at[block], out_ref.at[owner * capacity + rank])], sems.at[pl.ds(2 + block, 1)])
    for copy in copies:
        copy.wait()


def act_kernel(groups, chunk, gate_ref, up_ref, first_ref, second_ref, padded_ref, low_ref, mine_ref, gate, up, first, hidden, sems):
    rows, width = gate.shape
    per = width // groups
    step = 16
    pieces = [pl.ds(at, chunk) for at in range(0, rows, chunk)]
    coming = [
        fetch([(gate_ref.at[at, :], gate.at[at, :]), (up_ref.at[at, :], up.at[at, :])], sems.at[n])
        for n, at in enumerate(pieces)
    ]
    late = fetch([(first_ref, first), (second_ref.at[:, columns(0, mine_ref.shape[1])], mine_ref)], sems.at[len(pieces)])
    room = padded_ref.shape[2]
    for n, piece in enumerate(pieces):
        for copy in coming[n]:
            copy.wait()

        def one(index, carry, base=n * chunk):
            at = pl.ds(pl.multiple_of(base + index * step, step), step)
            gate_vals = gate[at, :].astype(F32)
            silu = gate_vals * jax.nn.sigmoid(gate_vals)
            hidden[at, :] = (silu * up[at, :].astype(F32)).astype(BF16)
            return carry

        lax.fori_loop(0, chunk // step, one, 0)
    for copy in late:
        copy.wait()
    low_ref[...] = dot(hidden[...], first[...], NT)
    for group in range(groups):
        padded_ref[group, :, pl.ds(0, per)] = hidden[:, group * per : (group + 1) * per]
        if room > per:
            padded_ref[group, :, pl.ds(per, room - per)] = jnp.zeros((rows, room - per), BF16)


def shaped(shape, dtype):
    return jax.ShapeDtypeStruct(shape, dtype)


def columns(bit, width):
    return pl.ds(pl.multiple_of((lax.axis_index("mp") ^ bit) * width, LANES), width)


def through_kernel(own_ref, second_ref, out_ref):
    out_ref[...] = dot(own_ref[...], second_ref[...], NT)


def add_kernel(one_ref, other_ref, out_ref):
    out_ref[...] = (one_ref[...] + other_ref[...]).astype(out_ref.dtype)


def make_share(groups, brows, width, rank, per):
    _, _, _, _, q, r, blocks, share, _ = layout_of(rank, per, brows, width)

    def kernel(x_ref, low_a, low_b, out_ref, prod):
        low = (low_a[...] + low_b[...]).astype(BF16)
        prod[...] = dot(low, x_ref[...], TN)
        for group in range(groups):
            at = 0
            for j in range(blocks):
                for k in range(q):
                    out_ref[group, pl.ds(at, SUB), :] = prod[
                        pl.ds(group * brows + k * SUB, SUB), pl.ds(j * LANES, LANES)
                    ].astype(BF16)
                    at += SUB
            if r:
                for j in range(0, blocks, share):
                    pieces = [
                        prod[pl.ds(group * brows + q * SUB, r), pl.ds(i * LANES, LANES)]
                        for i in range(j, min(j + share, blocks))
                    ]
                    lack = SUB - r * len(pieces)
                    if lack:
                        pieces.append(jnp.zeros((lack, LANES), F32))
                    out_ref[group, pl.ds(at, SUB), :] = jnp.concatenate(pieces, 0).astype(BF16)
                    at += SUB

    return kernel


def make_send(groups, brows, width, rank, per):
    full_, rem, half, a_rows, _, _, _, _, b_rows = layout_of(rank, per, brows, width)

    def kernel(pair_0, pair_1, padded_ref, share_ref, through_ref, *outs):
        through = (pair_0[...].astype(F32) + pair_1[...].astype(F32)).astype(BF16)
        through_ref[...] = through
        for peer, out_ref in enumerate(outs):
            for side in range(2):
                group = lax.axis_index("dp") ^ (peer + side * len(outs))
                piece = dot(through, padded_ref[group], TN)
                for j in range(full_):
                    out_ref[side, pl.ds(j * rank, rank), :] = piece[:, j * LANES : (j + 1) * LANES].astype(BF16)
                if rem:
                    last = piece[:, full_ * LANES : (full_ + 1) * LANES]
                    if half:
                        last = last[: rank // 2] + pltpu.roll(last[rank // 2 :], LANES // 2, 1)
                    out_ref[side, pl.ds(full_ * rank, last.shape[0]), :] = last.astype(BF16)
                out_ref[side, pl.ds(a_rows, b_rows), :] = share_ref[group]

    return kernel


def make_half(groups, brows, width, rank, per):
    _, _, _, a_rows, _, _, _, _, _ = layout_of(rank, per, brows, width)

    def kernel(*refs):
        *parts, mine_ref, other_ref, b_ref = refs
        for side in range(2):
            total = parts[0][side].astype(F32)
            for part in parts[1:]:
                total = total + part[side].astype(F32)
            b_ref[side] = total[a_rows:].astype(BF16)
            if side:
                other_ref[...] = total[:a_rows].astype(BF16)
            else:
                mine_ref[...] = total[:a_rows]

    return kernel


def gather_kernel(*refs):
    *parts, out_ref = refs
    for at, part in enumerate(parts):
        out_ref[at] = part[1]


def make_finish(groups, brows, width, rank, per):
    full_, rem, half, _, q, r, blocks, share, _ = layout_of(rank, per, brows, width)

    def kernel(mine_ref, other_ref, own_ref, core_ref, x_ref, far_ref, landed_ref, a_ref, b_ref, total, part):
        total[...] = mine_ref[...] + other_ref[...].astype(F32)
        for j in range(full_):
            a_ref[0, :, pl.ds(j * LANES, LANES)] = total[pl.ds(j * rank, rank), :]
        if rem:
            at = pl.ds(full_ * LANES, rem)
            if half:
                last = total[pl.ds(full_ * rank, rank // 2), :]
                a_ref[0, pl.ds(0, rank // 2), at] = last[:, :rem]
                a_ref[0, pl.ds(rank // 2, rank // 2), at] = pltpu.roll(last, LANES // 2, 1)[:, :rem]
            else:
                a_ref[0, :, at] = total[pl.ds(full_ * rank, rank), :][:, :rem]
        for bit, ref in enumerate((own_ref, core_ref, x_ref, far_ref)):
            part[...] = ref[0].astype(F32) + landed_ref[bit].astype(F32)
            base = (lax.axis_index("mp") ^ bit) * width
            at = 0
            for j in range(blocks):
                cols = pl.ds(pl.multiple_of(base + j * LANES, LANES), LANES)
                for k in range(q):
                    b_ref[pl.ds(k * SUB, SUB), cols] = part[pl.ds(at, SUB), :]
                    at += SUB
            if r:
                for j in range(0, blocks, share):
                    for i in range(j, min(j + share, blocks)):
                        cols = pl.ds(pl.multiple_of(base + i * LANES, LANES), LANES)
                        b_ref[pl.ds(q * SUB, r), cols] = part[pl.ds(at + (i - j) * r, r), :]
                    at += SUB

    return kernel


def near_kernel(
    tile, first_ref, weight_ref, own_ref, core_ref, through_ref, out_ref, first, weight, total, arrive, leave
):
    hid = weight_ref.shape[0]
    width = own_ref.shape[1]
    spans = [pl.ds(at, min(tile, hid - at)) for at in range(0, hid, tile)]
    coming = fetch([(weight_ref.at[:, columns(bit, width)], weight.at[bit]) for bit in range(2)], arrive)
    small = fetch([(first_ref, first)], arrive.at[pl.ds(2, 1)])
    small[0].wait()
    for span in spans:
        total[:, span] = dot(through_ref[...], first[:, span], (((1,), (0,)), ((), ())))
    leaving = []
    for bit, ref in enumerate((own_ref, core_ref)):
        coming[bit].wait()
        for index, span in enumerate(spans):
            total[:, span] += dot(ref[...], weight[bit, span], NT)
            if bit:
                leaving += fetch([(total.at[:, span], out_ref.at[:, span])], leave.at[pl.ds(index, 1)])
    for copy in leaving:
        copy.wait()


def distant_kernel(
    tile, weight_ref, total_ref, gate_in, up_in, x_ref, far_ref, gate_ref, up_ref,
    weight, total, gate, up, grad_gate, grad_up, arrive, leave,
):
    hid = weight_ref.shape[0]
    width = x_ref.shape[1]
    spans = [pl.ds(at, min(tile, hid - at)) for at in range(0, hid, tile)]
    coming = fetch(
        [
            (weight_ref.at[:, columns(2, width)], weight.at[0]),
            (total_ref, total),
            (weight_ref.at[:, columns(3, width)], weight.at[1]),
            (gate_in, gate),
            (up_in, up),
        ],
        arrive,
    )
    leaving = []
    coming[0].wait()
    coming[1].wait()
    for span in spans:
        total[:, span] += dot(x_ref[...], weight[0, span], NT)
    for copy in coming[2:]:
        copy.wait()
    for index, span in enumerate(spans):
        acc = total[:, span] + dot(far_ref[...], weight[1, span], NT)
        gate_vals = gate[:, span].astype(F32)
        sig = jax.nn.sigmoid(gate_vals)
        slope = up[:, span].astype(F32) * sig * (1.0 + gate_vals * (1.0 - sig))
        grad_gate[:, span] = (acc * slope).astype(BF16)
        grad_up[:, span] = (acc * (gate_vals * sig)).astype(BF16)
        leaving += fetch([(grad_gate.at[:, span], gate_ref.at[:, span]), (grad_up.at[:, span], up_ref.at[:, span])], leave.at[index])
    for copy in leaving:
        copy.wait()


def near_call(own, core, through, first_t, weight, tile=512):
    rows, width = own.shape
    hid = weight.shape[0]
    rank = through.shape[1]
    return call(
        functools.partial(near_kernel, tile),
        [shaped((rows, hid), F32)],
        hbm=[first_t, weight],
        args=[own, core, through],
        flops=4 * rows * hid * width,
        scratch=[
            pltpu.VMEM((rank, hid), BF16),
            pltpu.VMEM((2, hid, width), BF16),
            pltpu.VMEM((rows, hid), F32),
            pltpu.SemaphoreType.DMA((3,)),
            pltpu.SemaphoreType.DMA((-(-hid // tile),)),
        ],
        room=ROOM,
        hbm_outs=1,
    )


def distant_call(total, other, far, weight, gate, up, tile=512):
    rows, width = other.shape
    hid = weight.shape[0]
    return call(
        functools.partial(distant_kernel, tile),
        [shaped((rows, hid), BF16)] * 2,
        hbm=[weight, total, gate, up],
        args=[other, far],
        flops=4 * rows * hid * width,
        scratch=[
            pltpu.VMEM((2, hid, width), BF16),
            pltpu.VMEM((rows, hid), F32),
            *[pltpu.VMEM((rows, hid), BF16)] * 4,
            pltpu.SemaphoreType.DMA((5,)),
            pltpu.SemaphoreType.DMA((-(-hid // tile), 2)),
        ],
        room=ROOM,
        hbm_outs=2,
    )


def swap(value, bit):
    count = lax.axis_size("mp")
    return lax.ppermute(value, "mp", [(i, i ^ bit) for i in range(count)])


def trade(value, bit):
    count = lax.axis_size("dp")
    return lax.ppermute(value, "dp", [(i, i ^ bit) for i in range(count)])


def fast_body(*args):
    return fast_layer(*args)


def fast_layer(output_gradient, gate_preactivation, up_preactivation, down_weight, adapter_first, adapter_second, plan):
    groups = lax.axis_size("dp")
    owned = plan.shape[0]
    capacity = owned // groups
    tokens, width = output_gradient.shape
    hid, rank = adapter_first.shape
    per, brows = hid // groups, rank // groups
    tall = tokens // owned
    first_t = adapter_first.T
    room = -(-per // LANES) * LANES
    _, _, _, a_rows, _, _, _, _, b_rows = layout_of(rank, per, brows, width)
    sizes = (groups, brows, width, rank, per)

    outgoing = call(
        functools.partial(pack_kernel, capacity),
        [shaped((owned, tall, width), BF16)],
        hbm=[plan, output_gradient.reshape(owned, tall, width)],
        scratch=[
            pltpu.VMEM((owned, tall, width), BF16),
            pltpu.SMEM((owned,), jnp.int32),
            pltpu.SMEM((groups,), jnp.int32),
            pltpu.SemaphoreType.DMA((owned + 2,)),
        ],
        room=0,
        hbm_outs=1,
    )
    packed = lax.all_to_all(outgoing, "dp", split_axis=0, concat_axis=0, tiled=True).reshape(tokens, width)

    chunk = tokens // 4 if tokens % 64 == 0 else tokens
    padded, low_0, second = call(
        functools.partial(act_kernel, groups, chunk),
        [
            shaped((groups, tokens, room), BF16),
            shaped((tokens, rank), F32),
            shaped((rank, width), BF16),
        ],
        hbm=[gate_preactivation, up_preactivation, first_t, adapter_second],
        flops=2 * tokens * hid * rank,
        scratch=[
            pltpu.VMEM((tokens, hid), BF16),
            pltpu.VMEM((tokens, hid), BF16),
            pltpu.VMEM((rank, hid), BF16),
            pltpu.VMEM((tokens, hid), BF16),
            pltpu.SemaphoreType.DMA((tokens // chunk + 1, 2)),
        ],
        room=11000,
    )
    low_1 = swap(low_0, 1)
    low_a = call(add_kernel, [shaped((tokens, rank), F32)], args=[low_0, low_1])
    low_b = swap(low_a, 2)

    part_0 = call(through_kernel, [shaped((tokens, rank), F32)], args=[packed, second], flops=2 * tokens * width * rank)
    part_1 = swap(part_0, 1)
    pair_0 = call(add_kernel, [shaped((tokens, rank), BF16)], args=[part_0, part_1])
    pair_1 = swap(pair_0, 2)
    share = call(
        make_share(*sizes),
        [shaped((groups, b_rows, LANES), BF16)],
        args=[packed, low_a, low_b],
        scratch=[pltpu.VMEM((rank, width), F32)],
    )
    side = swap(packed, 2)
    core = swap(packed, 1)

    peers = groups // 2
    through, *payload = call(
        make_send(*sizes),
        [shaped((tokens, rank), BF16)] + [shaped((2, a_rows + b_rows, LANES), BF16)] * peers,
        args=[pair_0, pair_1, padded, share],
        flops=2 * tokens * hid * rank,
    )
    arrived = [payload[0]]
    for peer in range(1, peers):
        arrived.append(trade(payload[peer], peer))

    total = near_call(packed, core, through, first_t, down_weight)
    mine, other, b_0 = call(
        make_half(*sizes),
        [shaped((a_rows, LANES), F32), shaped((a_rows, LANES), BF16), shaped((2, b_rows, LANES), BF16)],
        args=arrived,
    )
    b_3 = swap(b_0, 3)
    b_2 = swap(b_0, 2)
    b_1 = swap(b_0, 1)
    landed = trade(other, peers)
    far = swap(side, 1)
    b_all = call(gather_kernel, [shaped((4, b_rows, LANES), BF16)], args=[b_0, b_1, b_2, b_3])
    b_landed = trade(b_all, peers)
    grad_gate, grad_up = distant_call(total, side, far, down_weight, gate_preactivation, up_preactivation)
    grad_a_t, grad_b = call(
        make_finish(*sizes),
        [shaped((1, rank, per), F32), shaped((brows, 4 * width), F32)],
        args=[mine, landed, b_0, b_1, b_2, b_3, b_landed],
        scratch=[pltpu.VMEM((a_rows, LANES), F32), pltpu.VMEM((b_rows, LANES), F32)],
    )
    return grad_gate, grad_up, jnp.swapaxes(grad_a_t, 1, 2), grad_b


def general_body(
    output_gradient,
    gate_preactivation,
    up_preactivation,
    down_weight,
    adapter_first,
    adapter_second,
    plan,
):
    groups = lax.axis_size("dp")
    owned = plan.shape[0]
    capacity = -(-owned // groups)
    tokens_here = output_gradient.shape[0]
    feature_cols = output_gradient.shape[1]
    block_width = tokens_here // owned * feature_cols
    slot_count = groups * capacity
    positions = jnp.arange(owned, dtype=jnp.int32)
    earlier = (plan[None, :] == plan[:, None]) & (positions[None, :] < positions[:, None])
    target = plan * capacity + jnp.sum(earlier.astype(jnp.int32), axis=1)
    sending = target[None, :] == jnp.arange(slot_count, dtype=jnp.int32)[:, None]
    outgoing = jnp.dot(
        sending.astype(jnp.bfloat16),
        output_gradient.reshape(owned, block_width),
        preferred_element_type=jnp.float32,
    ).astype(jnp.bfloat16)
    filled = jnp.sum(sending.astype(jnp.float32), axis=1).astype(jnp.bfloat16)
    arrived, present = (
        lax.all_to_all(outgoing, "dp", split_axis=0, concat_axis=0, tiled=True),
        lax.all_to_all(filled, "dp", split_axis=0, concat_axis=0, tiled=True),
    )
    present_flag = present.astype(jnp.int32)
    ranking = jnp.cumsum(present_flag) - 1
    keeping = (ranking[None, :] == positions[:, None]) & (present_flag[None, :] > 0)
    packed_tokens = (
        jnp.dot(keeping.astype(jnp.bfloat16), arrived, preferred_element_type=jnp.float32)
        .astype(jnp.bfloat16)
        .reshape(tokens_here, feature_cols)
    )
    feature_rows = lax.all_gather(packed_tokens, "mp", axis=1, tiled=True)
    gate_vals = gate_preactivation.astype(jnp.float32)
    up_vals = up_preactivation.astype(jnp.float32)
    sigmoid_gate = jax.nn.sigmoid(gate_vals)
    silu_gate = gate_vals * sigmoid_gate
    hidden_units = (silu_gate * up_vals).astype(jnp.bfloat16)
    low_rank_piece = jnp.dot(hidden_units, adapter_first, preferred_element_type=jnp.float32)
    low_rank_rows = lax.psum(low_rank_piece, "mp").astype(jnp.bfloat16)
    passed_through = lax.dot_general(
        feature_rows, adapter_second, (((1,), (1,)), ((), ())), preferred_element_type=jnp.float32
    ).astype(jnp.bfloat16)
    grad_a_rows = lax.psum_scatter(
        lax.dot_general(
            hidden_units,
            passed_through,
            (((0,), (0,)), ((), ())),
            preferred_element_type=jnp.float32,
        ),
        "dp",
        scatter_dimension=0,
        tiled=True,
    )
    part_rows = lax.psum_scatter(
        lax.dot_general(
            low_rank_rows,
            packed_tokens,
            (((0,), (0,)), ((), ())),
            preferred_element_type=jnp.float32,
        ),
        "dp",
        scatter_dimension=0,
        tiled=True,
    )
    grad_b_rows = lax.all_gather(part_rows, "mp", axis=1, tiled=True)
    hidden_gradient = lax.dot_general(
        feature_rows, down_weight, (((1,), (1,)), ((), ())), preferred_element_type=jnp.float32
    )
    hidden_gradient = hidden_gradient + lax.dot_general(
        passed_through, adapter_first, (((1,), (1,)), ((), ())), preferred_element_type=jnp.float32
    )
    grad_gate = (
        hidden_gradient * up_vals * sigmoid_gate * (1.0 + gate_vals * (1.0 - sigmoid_gate))
    ).astype(jnp.bfloat16)
    grad_up = (hidden_gradient * silu_gate).astype(jnp.bfloat16)
    return (grad_gate, grad_up, grad_a_rows[None], grad_b_rows)


def fits(mesh, args):
    groups, parts = mesh.shape["dp"], mesh.shape["mp"]
    gradient, _, _, _, first, _, plan = args
    owned = plan.shape[0] // groups
    tokens, width = gradient.shape[0] // groups, gradient.shape[1] // parts
    hid, rank = first.shape[0] // parts, first.shape[1]
    return (
        parts == 4
        and groups > 4 and groups & (groups - 1) == 0
        and owned % groups == 0
        and tokens == owned * SUB
        and tokens % 16 == 0
        and width % LANES == 0
        and hid % groups == 0
        and rank % groups == 0
        and rank % (2 * SUB) == 0
        and SUB % max(rank // groups % SUB, 1) == 0
    )


def solution(mesh):
    def step(*args):
        fast = fits(mesh, args)
        run = jax.shard_map(
            fast_body if fast else general_body,
            mesh=mesh,
            in_specs=(
                P("dp", "mp"),
                P("dp", "mp"),
                P("dp", "mp"),
                P("mp", None),
                P("mp", None),
                P(),
                P("dp"),
            ),
            out_specs=(P("dp", "mp"), P("dp", "mp"), P("mp", "dp", None), P("dp", None)),
            check_vma=False,
        )
        return run(*args)

    return step
```
